32 devices in a mesh: seq: 4 (over y, core), shard: 8 (over z, x).
Axes of the slice: x: 2, y: 2, z: 4, core: 2. Of those that a mesh axis runs over, the one named last changes fastest.
Arguments:
- frames: bfloat16 [8, 1024, 1536], P('shard', 'seq'), may hold values from -6 to 6
- text_states: bfloat16 [8, 64, 1536], P('shard', 'seq'), may hold values from -6 to 6
- holds_clip: int32 [8], P('shard'), may hold values 0 or 1
- self_proj: float32 [1536, 4608], P('shard'), may hold values from -0.15625 to 0.15625
- self_out: float32 [1536, 1536], P('shard'), may hold values from -0.625 to 0.625
- cross_query: float32 [1536, 1536], P('shard'), may hold values from -0.15625 to 0.15625
- cross_keyval: float32 [1536, 3072], P('shard'), may hold values from -0.15625 to 0.15625
- cross_out: float32 [1536, 1536], P('shard'), may hold values from -0.3125 to 0.3125
- feed_in: float32 [1536, 6144], P('shard'), may hold values from -0.15625 to 0.15625
- feed_out: float32 [6144, 1536], P('shard'), may hold values from -0.078125 to 0.078125
- norm_gain: float32 [3, 1536], P(None, 'shard'), may hold values from 0.5 to 1.5
- norm_bias: float32 [3, 1536], P(None, 'shard'), may hold values from -3 to 3
- cotangent: bfloat16 [8, 1024, 1536], P('shard', 'seq'), may hold values from -6 to 6
Outputs:
- block_out: bfloat16 [8, 1024, 1536], P('shard', 'seq')
- frames_grad: float32 [8, 1024, 1536], P('shard', 'seq')
- text_grad: float32 [8, 64, 1536], P('shard', 'seq')
- self_proj_grad: float32 [1536, 4608], P('shard')
- self_out_grad: float32 [1536, 1536], P('shard')
- cross_query_grad: float32 [1536, 1536], P('shard')
- cross_keyval_grad: float32 [1536, 3072], P('shard')
- cross_out_grad: float32 [1536, 1536], P('shard')
- feed_in_grad: float32 [1536, 6144], P('shard')
- feed_out_grad: float32 [6144, 1536], P('shard')
- norm_gain_grad: float32 [3, 1536], P(None, 'shard')
- norm_bias_grad: float32 [3, 1536], P(None, 'shard')
The draws below stay inside these ranges and needn't reach their ends.
Inputs may be any that keep to these rules, and one draw needn't show every extreme that they name: `holds_clip`: 1 where the slot holds a clip, 0 where it is empty.
All inputs are finite; a program needn't handle non-finite values. No bound on the sum of `holds_clip` on one device may be relied on, other than what follows from the above.
Results may differ from the reference program's by a relative error of at most 0.019.
Values may be sent and summed in bfloat16 or wider, within the bound.
No kernel may reach another device: no remote copies, remote signals or barrier semaphores. Data moves between devices by JAX's collectives and lax.ppermute only.
A program may use at most 384 MiB of HBM per device.

```python
import jax
import jax.numpy as jnp
from jax import lax

D = 1536
HEADS = 24
HEAD = 64
FF = 6144
TEXT = 64
LEN = 1024
GROUPS = 8


def touch_ends(array, stream_key, low, high):
    spot = [jax.random.randint(jax.random.fold_in(stream_key, axis), (), 0, length) for axis, length in enumerate(array.shape)]
    longest = array.shape.index(max(array.shape))
    beside = spot[:longest] + [(spot[longest] + 1) % array.shape[longest]] + spot[longest + 1:]
    return array.at[tuple(spot)].set(low).at[tuple(beside)].set(high)


def block_levels(stream_key, dims, shards, smallest, top_value):
    factor_of = 1.0
    for axis_at, blocks in shards:
        steps = jax.random.uniform(jax.random.fold_in(jax.random.fold_in(stream_key, 6), axis_at), (blocks,), jnp.float32, smallest / len(shards), top_value / len(shards))
        factor_of = factor_of * jnp.repeat(jnp.exp(steps), dims[axis_at] // blocks).reshape((-1,) + (1,) * (len(dims) - 1 - axis_at))
    return factor_of


def bell_draw(stream_key, dims, scale, limit, cuts=(), kind=jnp.bfloat16):
    values = scale * jax.random.normal(stream_key, dims, jnp.float32)
    if cuts:
        values = values * block_levels(stream_key, dims, cuts, -0.22, 0.18)
    return jnp.clip(values, -limit, limit).astype(kind)


def setup_inputs(seed: int = 0) -> dict:
    splits = jax.random.split(jax.random.key(seed), 14)
    frames = bell_draw(splits[0], (GROUPS, LEN, D), 1.0, 6.0, ((0, 8), (1, 4)))
    text_states = bell_draw(splits[1], (GROUPS, TEXT, D), 1.0, 6.0, ((0, 8), (1, 4)))
    holds_clip = touch_ends((jax.random.randint(splits[2], (GROUPS,), 0, 32) < 17).astype(jnp.int32), jax.random.fold_in(splits[2], 1), 0, 1)
    self_proj = bell_draw(splits[3], (D, 3 * D), D ** -0.5, 0.15625, ((0, 8),), jnp.float32)
    self_out = bell_draw(splits[4], (D, D), (D // 16) ** -0.5, 0.625, ((0, 8),), jnp.float32)
    cross_query = bell_draw(splits[5], (D, D), D ** -0.5, 0.15625, ((0, 8),), jnp.float32)
    cross_keyval = bell_draw(splits[6], (D, 2 * D), D ** -0.5, 0.15625, ((0, 8),), jnp.float32)
    cross_out = bell_draw(splits[7], (D, D), (D // 4) ** -0.5, 0.3125, ((0, 8),), jnp.float32)
    feed_in = bell_draw(splits[8], (D, FF), D ** -0.5, 0.15625, ((0, 8),), jnp.float32)
    feed_out = bell_draw(splits[9], (FF, D), FF ** -0.5, 0.078125, ((0, 8),), jnp.float32)
    norm_gain = jnp.clip(1.0 + 0.1 * jax.random.normal(splits[10], (3, D), jnp.float32), 0.5, 1.5)
    norm_bias = bell_draw(splits[11], (3, D), 0.5, 3.0, ((1, 8),), jnp.float32)
    cotangent = bell_draw(splits[12], (GROUPS, LEN, D), 1.0, 6.0, ((0, 8), (1, 4)))
    return {"frames": frames, "text_states": text_states, "holds_clip": holds_clip, "self_proj": self_proj, "self_out": self_out, "cross_query": cross_query, "cross_keyval": cross_keyval, "cross_out": cross_out, "feed_in": feed_in, "feed_out": feed_out, "norm_gain": norm_gain, "norm_bias": norm_bias, "cotangent": cotangent}


@jax.custom_vjp
def low(v):
    return lax.optimization_barrier(v.astype(jnp.bfloat16)).astype(jnp.float32)

@jax.custom_vjp
def low_back(v):
    return v

def low_keep(v):
    return (low(v), None)

def low_pass(kept, grad):
    return (grad,)

def back_keep(v):
    return (v, None)

def back_low(kept, grad):
    return (low(grad),)
low.defvjp(low_keep, low_pass)
low_back.defvjp(back_keep, back_low)
EPSILON = 1e-05
MASKED = -1e+30
HIGHEST = lax.Precision.HIGHEST

def layer_norm(values, gain_row, shift_row):
    centre = values - lax.optimization_barrier(jnp.mean(values, axis=-1, keepdims=True))
    spread = lax.optimization_barrier(jnp.mean(centre * centre, axis=-1, keepdims=True))
    return centre * lax.rsqrt(spread + EPSILON) * gain_row + shift_row

def product(left, right):
    return jnp.dot(left, right, precision=HIGHEST)

def decoder_layer(params, clip_frames, clip_text):
    rounded = [low(member) for member in params]
    proj_weight, out_weight, query_weight, keyval_weight, cross_weight, expand_weight, contract_weight, gains, shifts = rounded
    length = clip_frames.shape[0]
    factor = HEAD ** (-0.5)
    normed_one = layer_norm(clip_frames, gains[0], shifts[0])
    packed = low_back(low(product(low(normed_one), proj_weight))).reshape(length, 3, HEADS, HEAD)
    scores = jnp.einsum('qhd,khd->hqk', packed[:, 0], packed[:, 1], precision=HIGHEST) * factor
    query_pos = lax.broadcasted_iota(jnp.int32, scores.shape, 1)
    key_pos = lax.broadcasted_iota(jnp.int32, scores.shape, 2)
    scores = jnp.where(key_pos <= query_pos, low_back(scores), MASKED)
    attention = jax.nn.softmax(scores, axis=-1)
    heads_out = jnp.einsum('hqk,khd->qhd', low(attention), packed[:, 2], precision=HIGHEST)
    heads_out = low_back(low(heads_out.reshape(length, HEADS * HEAD)))
    mixed_one = clip_frames + low_back(product(heads_out, out_weight))
    normed_two = layer_norm(mixed_one, gains[1], shifts[1])
    cross_queries = low_back(low(product(low(normed_two), query_weight))).reshape(length, HEADS, HEAD)
    text_pairs = low_back(low(product(clip_text, keyval_weight))).reshape(TEXT, 2, HEADS, HEAD)
    cross_scores = low_back(jnp.einsum('qhd,khd->hqk', cross_queries, text_pairs[:, 0], precision=HIGHEST) * factor)
    cross_attention = jax.nn.softmax(cross_scores, axis=-1)
    cross_heads = jnp.einsum('hqk,khd->qhd', low(cross_attention), text_pairs[:, 1], precision=HIGHEST)
    cross_heads = low_back(low(cross_heads.reshape(length, HEADS * HEAD)))
    mixed_two = mixed_one + low_back(product(cross_heads, cross_weight))
    normed_three = layer_norm(mixed_two, gains[2], shifts[2])
    hidden_pre = low_back(product(low(normed_three), expand_weight))
    hidden = low(jax.nn.gelu(hidden_pre, approximate=False))
    return mixed_two + low_back(product(hidden, contract_weight))

def reference(frames, text_states, holds_clip, self_proj, self_out, cross_query, cross_keyval, cross_out, feed_in, feed_out, norm_gain, norm_bias, cotangent):
    params = (self_proj, self_out, cross_query, cross_keyval, cross_out, feed_in, feed_out, norm_gain, norm_bias)
    params = tuple((member.astype(jnp.float32) for member in params))
    zeroed = tuple((jnp.zeros(member.shape, jnp.float32) for member in params))

    def one_clip(running, inputs_now):
        clip_frames, clip_text, presence, clip_cotan = inputs_now
        result, pull = jax.vjp(decoder_layer, params, clip_frames.astype(jnp.float32), clip_text.astype(jnp.float32))
        weight_grads, clip_grad, text_part = pull(clip_cotan.astype(jnp.float32) * presence)
        running = jax.tree.map(jnp.add, running, weight_grads)
        return (running, ((result * presence).astype(jnp.bfloat16), clip_grad, text_part))
    totals, outputs = lax.scan(one_clip, zeroed, (frames, text_states, holds_clip.astype(jnp.float32), cotangent))
    block_out, frames_grad, text_grad = outputs
    return (block_out, frames_grad, text_grad, totals[0], totals[1], totals[2], totals[3], totals[4], totals[5], totals[6], totals[7], totals[8])
```

```python
import jax
import jax.numpy as jnp
from jax import lax
from jax.sharding import PartitionSpec as P

HEADS = 24
HEAD = 64


EPSILON = 1e-05
MASKED = -1e30


def layer_norm(values, gain_row, shift_row):
    centre = values - jnp.mean(values, axis=-1, keepdims=True)
    spread = jnp.mean(centre * centre, axis=-1, keepdims=True)
    return centre * lax.rsqrt(spread + EPSILON) * gain_row + shift_row


def gelu_exact(values):
    return jax.nn.gelu(values, approximate=False)


def product(left, right):
    return jnp.dot(left, right, preferred_element_type=jnp.float32)


def transposed_left(left, right):
    return lax.dot_general(
        left, right, (((0,), (0,)), ((), ())), preferred_element_type=jnp.float32
    )


def transposed_right(left, right):
    return lax.dot_general(
        left, right, (((1,), (1,)), ((), ())), preferred_element_type=jnp.float32
    )


def low(values):
    return values.astype(jnp.bfloat16)


def swap(values, bit, axis="seq"):
    count = lax.axis_size(axis)
    return lax.ppermute(values, axis, [(i, i ^ bit) for i in range(count)])


def by_index(blocks):
    own = lax.axis_index("seq")
    core = (own & 1) == 1
    chip = (own & 2) == 2
    near = [
        jnp.where(core, blocks[1], blocks[0]),
        jnp.where(core, blocks[0], blocks[1]),
        jnp.where(core, blocks[3], blocks[2]),
        jnp.where(core, blocks[2], blocks[3]),
    ]
    return [
        jnp.where(chip, near[2], near[0]),
        jnp.where(chip, near[3], near[1]),
        jnp.where(chip, near[0], near[2]),
        jnp.where(chip, near[1], near[3]),
    ]


def seq_gather(values):
    far = swap(values, 2)
    return [values, swap(values, 1), far, swap(far, 1)]


def seq_reduce(parts, kind=jnp.bfloat16):
    beside = swap(parts[3].astype(kind), 1)
    across = swap((parts[2] + beside.astype(jnp.float32)).astype(kind), 2)
    close = swap(parts[1].astype(kind), 1)
    return parts[0] + close.astype(jnp.float32) + across.astype(jnp.float32)


def seq_exchange(blocks):
    return [blocks[0], swap(blocks[1], 1), swap(blocks[2], 2), swap(blocks[3], 3)]


def lines():
    count = lax.axis_size("shard")
    return [list(range(parity, count, 2)) for parity in range(2)]


def shard_gather(piece):
    line = lax.all_gather(piece, "shard", axis=0, axis_index_groups=lines())
    other = swap(line, 1, "shard")
    odd = (lax.axis_index("shard") & 1) == 1
    pair = jnp.stack([jnp.where(odd, other, line), jnp.where(odd, line, other)], axis=1)
    return pair.reshape((-1,) + piece.shape)


def shard_reduce(terms):
    pair = terms.reshape((-1, 2) + terms.shape[1:])
    parity = lax.axis_index("shard") & 1
    away = lax.dynamic_index_in_dim(pair, 1 - parity, 1, keepdims=False)
    mine = lax.dynamic_index_in_dim(pair, parity, 1, keepdims=False)
    came = swap(away, 1, "shard")
    total = low(mine.astype(jnp.float32) + came.astype(jnp.float32))
    flat = total.reshape((-1,) + total.shape[2:])
    return lax.psum_scatter(
        flat, "shard", scatter_dimension=0, tiled=True, axis_index_groups=lines()
    )


def causal_scores(query_block, key_prefix, offset):
    scores = jnp.einsum(
        "qhd,khd->hqk", query_block, key_prefix, preferred_element_type=jnp.float32
    ) * HEAD ** (-0.5)
    query_pos = offset + lax.broadcasted_iota(jnp.int32, scores.shape, 1)
    key_pos = lax.broadcasted_iota(jnp.int32, scores.shape, 2)
    return jnp.where(key_pos <= query_pos, scores, MASKED)


def causal_forward(query_heads, key_heads, value_heads):
    length = query_heads.shape[0]
    block_rows = min(512, length)
    outputs = []
    log_sums = []
    for first_row in range(0, length, block_rows):
        last_row = first_row + block_rows
        scores = causal_scores(query_heads[first_row:last_row], key_heads[:last_row], first_row)
        row_peak = jnp.max(scores, axis=-1, keepdims=True)
        expd = jnp.exp(scores - row_peak)
        row_total = jnp.sum(expd, axis=-1, keepdims=True)
        probabilities = (expd / row_total).astype(jnp.bfloat16)
        outputs.append(
            jnp.einsum(
                "hqk,khd->qhd",
                probabilities,
                value_heads[:last_row],
                preferred_element_type=jnp.float32,
            )
        )
        log_sums.append(row_peak + jnp.log(row_total))
    return (jnp.concatenate(outputs, axis=0).astype(jnp.bfloat16), log_sums)


def causal_backward(query_heads, key_heads, value_heads, grad_heads, log_sums):
    length = query_heads.shape[0]
    block_rows = min(512, length)
    factor = HEAD ** (-0.5)
    query_grads = []
    key_grads = jnp.zeros(key_heads.shape, jnp.float32)
    value_grads = jnp.zeros(value_heads.shape, jnp.float32)
    for block_index, first_row in enumerate(range(0, length, block_rows)):
        last_row = first_row + block_rows
        query_block = query_heads[first_row:last_row]
        grad_block = grad_heads[first_row:last_row]
        scores = causal_scores(query_block, key_heads[:last_row], first_row)
        probabilities = jnp.exp(scores - log_sums[block_index])
        grad_probs = jnp.einsum(
            "qhd,khd->hqk", grad_block, value_heads[:last_row], preferred_element_type=jnp.float32
        )
        row_inner = jnp.sum(probabilities * grad_probs, axis=-1, keepdims=True)
        grad_scores = (probabilities * (grad_probs - row_inner)).astype(jnp.bfloat16)
        query_grads.append(
            jnp.einsum(
                "hqk,khd->qhd",
                grad_scores,
                key_heads[:last_row],
                preferred_element_type=jnp.float32,
            )
            * factor
        )
        key_grads = key_grads.at[:last_row].add(
            jnp.einsum("hqk,qhd->khd", grad_scores, query_block, preferred_element_type=jnp.float32)
            * factor
        )
        value_grads = value_grads.at[:last_row].add(
            jnp.einsum(
                "hqk,qhd->khd",
                probabilities.astype(jnp.bfloat16),
                grad_block,
                preferred_element_type=jnp.float32,
            )
        )
    return (jnp.concatenate(query_grads, axis=0), key_grads, value_grads)


def on_device(
    frames,
    text_states,
    holds_clip,
    self_proj,
    self_out,
    cross_query,
    cross_keyval,
    cross_out,
    feed_in,
    feed_out,
    norm_gain,
    norm_bias,
    cotangent,
):
    seq_count = lax.axis_size("seq")
    shards = lax.axis_size("shard")
    own = lax.axis_index("seq")
    factor = HEAD ** (-0.5)
    presence = holds_clip.astype(jnp.float32)[0]
    inputs = frames[0].astype(jnp.float32)
    rows, width = inputs.shape
    group_width = width // seq_count
    head_group = group_width // HEAD
    length = rows * seq_count
    strip = self_proj.shape[0]
    units = feed_in.shape[1]
    unit_strip = units // (shards * seq_count)

    def columns(weight, parts):
        cut = weight.reshape(strip, parts, seq_count, -1)
        cut = lax.dynamic_index_in_dim(cut, own, 2, keepdims=False)
        return low(cut).reshape(strip, -1)

    def all_rows(piece):
        full = shard_gather(piece)
        return full.reshape(-1, piece.shape[1])

    norms = low(jnp.concatenate([norm_gain, norm_bias], axis=0))
    norms = lax.all_gather(norms, "shard", axis=1, tiled=True).astype(jnp.float32)
    gains, shifts = norms[:3], norms[3:]
    proj_own = all_rows(columns(self_proj, 3))
    squares = [columns(weight, 1) for weight in (self_out, cross_query, cross_out)]
    squares_own = all_rows(jnp.concatenate(squares, axis=1))
    keyval_own = all_rows(columns(cross_keyval, 2))
    expand_own = all_rows(columns(feed_in, shards))
    contract_piece = lax.dynamic_slice_in_dim(feed_out, own * unit_strip, unit_strip, 0)
    contract_own = all_rows(low(contract_piece))

    gathered = by_index(seq_gather(squares_own))
    out_full, query_full, cross_full = (
        jnp.concatenate(
            [block[:, i * group_width : (i + 1) * group_width] for block in gathered], axis=1
        )
        for i in range(3)
    )

    normed_one = low(layer_norm(inputs, gains[0], shifts[0]))
    normed_one_all = jnp.concatenate(seq_gather(normed_one), axis=0)
    packed = low(product(normed_one_all, proj_own)).reshape(seq_count, rows, 3 * group_width)
    packed = jnp.concatenate(by_index([packed[b] for b in range(seq_count)]), axis=0)
    packed = packed.reshape(length, 3, head_group, HEAD)
    query_heads, key_heads, value_heads = packed[:, 0], packed[:, 1], packed[:, 2]
    heads_out, log_sums = causal_forward(query_heads, key_heads, value_heads)
    heads_out = heads_out.reshape(seq_count, rows, group_width)
    heads_out = seq_exchange(by_index([heads_out[b] for b in range(seq_count)]))
    attn_rows = jnp.concatenate(by_index(heads_out), axis=1)
    mixed_one = inputs + product(attn_rows, out_full)

    text_rows = text_states[0]
    text_all = jnp.concatenate(by_index(seq_gather(text_rows)), axis=0)
    text_count = text_all.shape[0]
    pairs = by_index(seq_gather(low(product(text_all, keyval_own))))
    text_keys = jnp.concatenate([pair[:, :group_width] for pair in pairs], axis=1)
    text_values = jnp.concatenate([pair[:, group_width:] for pair in pairs], axis=1)
    text_keys = text_keys.reshape(text_count, HEADS, HEAD)
    text_values = text_values.reshape(text_count, HEADS, HEAD)
    normed_two = low(layer_norm(mixed_one, gains[1], shifts[1]))
    cross_queries = low(product(normed_two, query_full)).reshape(rows, HEADS, HEAD)
    cross_scores = (
        jnp.einsum("qhd,khd->hqk", cross_queries, text_keys, preferred_element_type=jnp.float32)
        * factor
    )
    row_peak = jnp.max(cross_scores, axis=-1, keepdims=True)
    expd = jnp.exp(cross_scores - row_peak)
    cross_probs = expd / jnp.sum(expd, axis=-1, keepdims=True)
    cross_rounded = low(cross_probs)
    cross_heads = low(
        jnp.einsum("hqk,khd->qhd", cross_rounded, text_values, preferred_element_type=jnp.float32)
    ).reshape(rows, width)
    mixed_two = mixed_one + product(cross_heads, cross_full)

    normed_three = low(layer_norm(mixed_two, gains[2], shifts[2]))
    blocks = seq_gather(normed_three)
    normed_three_all = [
        jnp.concatenate(blocks[:2], axis=0),
        jnp.concatenate(blocks[2:], axis=0),
    ]
    hidden_pre = [product(half, expand_own) for half in normed_three_all]
    hidden = [low(gelu_exact(half)) for half in hidden_pre]
    results = [product(half, contract_own) for half in hidden]
    parts = [results[0][:rows], results[0][rows:], results[1][:rows], results[1][rows:]]
    result = mixed_two + seq_reduce(parts)
    block_out = low(presence * result)[None]

    grad_block = low(presence * cotangent[0].astype(jnp.float32))
    grad_result = grad_block.astype(jnp.float32)
    blocks = seq_gather(grad_block)
    grad_block_all = [
        jnp.concatenate(blocks[:2], axis=0),
        jnp.concatenate(blocks[2:], axis=0),
    ]
    grad_pre = []
    for index in (0, 1):
        grad_hidden = transposed_right(grad_block_all[index], contract_own)
        gelu_pull = jax.vjp(gelu_exact, hidden_pre[index])[1]
        grad_pre.append(low(gelu_pull(grad_hidden)[0]))
    results = [transposed_right(half, expand_own) for half in grad_pre]
    parts = [results[0][:rows], results[0][rows:], results[1][:rows], results[1][rows:]]
    grad_normed = seq_reduce(parts)
    contract_term = transposed_left(
        jnp.concatenate(hidden, axis=0), jnp.concatenate(grad_block_all, axis=0)
    )
    expand_term = transposed_left(
        jnp.concatenate(normed_three_all, axis=0), jnp.concatenate(grad_pre, axis=0)
    )
    contract_share = shard_reduce(low(contract_term).reshape(shards, unit_strip, width))
    expand_share = shard_reduce(low(expand_term).reshape(shards, strip, -1))
    norm_pull = jax.vjp(layer_norm, mixed_two, gains[2], shifts[2])[1]
    grad_mixed, gain_three, shift_three = norm_pull(grad_normed)
    grad_two = grad_result + grad_mixed

    def square_share(left, right):
        cut = [right[:, j * group_width : (j + 1) * group_width] for j in range(seq_count)]
        cut = by_index(cut)
        quarter = seq_reduce([transposed_left(left, block) for block in cut])
        return shard_reduce(low(quarter).reshape(shards, strip, group_width))

    grad_cross = low(grad_two)
    cross_share = square_share(cross_heads, grad_cross)
    grad_heads_two = low(transposed_right(grad_cross, cross_full)).reshape(rows, HEADS, HEAD)
    grad_probs = jnp.einsum(
        "qhd,khd->hqk", grad_heads_two, text_values, preferred_element_type=jnp.float32
    )
    row_inner = jnp.sum(cross_probs * grad_probs, axis=-1, keepdims=True)
    grad_scores = low(cross_probs * (grad_probs - row_inner))
    grad_queries = low(
        jnp.einsum("hqk,khd->qhd", grad_scores, text_keys, preferred_element_type=jnp.float32)
        * factor
    ).reshape(rows, width)
    grad_text_keys = (
        jnp.einsum("hqk,qhd->khd", grad_scores, cross_queries, preferred_element_type=jnp.float32)
        * factor
    ).reshape(text_count, width)
    grad_text_values = jnp.einsum(
        "hqk,qhd->khd", cross_rounded, grad_heads_two, preferred_element_type=jnp.float32
    ).reshape(text_count, width)
    cut = [
        jnp.concatenate(
            [
                grad_text_keys[:, j * group_width : (j + 1) * group_width],
                grad_text_values[:, j * group_width : (j + 1) * group_width],
            ],
            axis=1,
        )
        for j in range(seq_count)
    ]
    own_pairs = low(seq_reduce(by_index(cut), jnp.float32))
    text_term = transposed_right(own_pairs, keyval_own).reshape(seq_count, -1, width)
    text_grad = seq_reduce(by_index([text_term[b] for b in range(seq_count)]), jnp.float32)[None]
    keyval_term = transposed_left(text_all, own_pairs)
    keyval_share = shard_reduce(low(keyval_term).reshape(shards, strip, -1))
    query_share = square_share(normed_two, grad_queries)
    norm_pull = jax.vjp(layer_norm, mixed_one, gains[1], shifts[1])[1]
    grad_mixed, gain_two, shift_two = norm_pull(transposed_right(grad_queries, query_full))
    grad_one = grad_two + grad_mixed

    grad_attn = low(grad_one)
    out_share = square_share(attn_rows, grad_attn)
    grad_rows = low(transposed_right(grad_attn, out_full))
    cut = [grad_rows[:, j * group_width : (j + 1) * group_width] for j in range(seq_count)]
    grad_heads = jnp.concatenate(by_index(seq_exchange(by_index(cut))), axis=0)
    grad_heads = grad_heads.reshape(length, head_group, HEAD)
    query_grad, key_grad, value_grad = causal_backward(
        query_heads, key_heads, value_heads, grad_heads, log_sums
    )
    grad_packed = low(jnp.stack([query_grad, key_grad, value_grad], axis=1))
    grad_packed = grad_packed.reshape(seq_count, rows, 3 * group_width)
    grad_packed = jnp.concatenate(by_index([grad_packed[b] for b in range(seq_count)]), axis=0)
    proj_term = transposed_left(normed_one_all, grad_packed)
    proj_share = shard_reduce(low(proj_term).reshape(shards, strip, -1))
    parts = transposed_right(grad_packed, proj_own).reshape(seq_count, rows, width)
    grad_normed = seq_reduce([parts[b] for b in range(seq_count)])
    norm_pull = jax.vjp(layer_norm, inputs, gains[0], shifts[0])[1]
    grad_mixed, gain_one, shift_one = norm_pull(grad_normed)
    frames_grad = (grad_one + grad_mixed)[None]

    norm_terms = jnp.stack([gain_one, gain_two, gain_three, shift_one, shift_two, shift_three])
    norm_terms = lax.psum(norm_terms, ("seq", "shard"))
    norm_terms = lax.dynamic_slice_in_dim(
        norm_terms, lax.axis_index("shard") * strip, strip, 1
    )

    def filled(share, parts):
        blocks = [block.reshape(strip, parts, 1, -1) for block in by_index(seq_gather(share))]
        return jnp.concatenate(blocks, axis=2).astype(jnp.float32).reshape(strip, -1)

    proj_grad = filled(proj_share, 3)
    out_grad = filled(out_share, 1)
    query_grad_w = filled(query_share, 1)
    keyval_grad = filled(keyval_share, 2)
    cross_grad = filled(cross_share, 1)
    feed_in_grad = filled(expand_share, shards)
    feed_out_grad = jnp.concatenate(by_index(seq_gather(contract_share)), axis=0).astype(
        jnp.float32
    )
    return (
        block_out,
        frames_grad,
        text_grad,
        proj_grad,
        out_grad,
        query_grad_w,
        keyval_grad,
        cross_grad,
        feed_in_grad,
        feed_out_grad,
        norm_terms[:3],
        norm_terms[3:],
    )


def solution(mesh):
    in_specs = (
        P("shard", "seq", None),
        P("shard", "seq", None),
        P("shard"),
        P("shard", None),
        P("shard", None),
        P("shard", None),
        P("shard", None),
        P("shard", None),
        P("shard", None),
        P("shard", None),
        P(None, "shard"),
        P(None, "shard"),
        P("shard", "seq", None),
    )
    out_specs = (
        P("shard", "seq", None),
        P("shard", "seq", None),
        P("shard", "seq", None),
        P("shard", None),
        P("shard", None),
        P("shard", None),
        P("shard", None),
        P("shard", None),
        P("shard", None),
        P("shard", None),
        P(None, "shard"),
        P(None, "shard"),
    )
    return jax.shard_map(
        on_device, mesh=mesh, in_specs=in_specs, out_specs=out_specs, check_vma=False
    )
```

```python
import jax
import jax.numpy as jnp
from jax import lax
from jax.sharding import PartitionSpec as P


HEADS = 24
HEAD = 64


EPSILON = 1e-05
MASKED = -1e30


def layer_norm(values, gain_row, shift_row):
    centre = values - jnp.mean(values, axis=-1, keepdims=True)
    spread = jnp.mean(centre * centre, axis=-1, keepdims=True)
    return centre * lax.rsqrt(spread + EPSILON) * gain_row + shift_row


def gelu_exact(values):
    return jax.nn.gelu(values, approximate=False)


def product(left, right):
    return jnp.dot(left, right, preferred_element_type=jnp.float32)


def transposed_left(left, right):
    return lax.dot_general(
        left, right, (((0,), (0,)), ((), ())), preferred_element_type=jnp.float32
    )


def transposed_right(left, right):
    return lax.dot_general(
        left, right, (((1,), (1,)), ((), ())), preferred_element_type=jnp.float32
    )


def low(values):
    return values.astype(jnp.bfloat16)


def swap(values, bit, axis="seq"):
    count = lax.axis_size(axis)
    return lax.ppermute(values, axis, [(i, i ^ bit) for i in range(count)])


def ring(values):
    count = lax.axis_size("shard")
    return lax.ppermute(values, "shard", [(i, (i + 2) % count) for i in range(count)])


def by_index(blocks):
    own = lax.axis_index("seq")
    core = (own & 1) == 1
    chip = (own & 2) == 2
    near = [
        jnp.where(core, blocks[1], blocks[0]),
        jnp.where(core, blocks[0], blocks[1]),
        jnp.where(core, blocks[3], blocks[2]),
        jnp.where(core, blocks[2], blocks[3]),
    ]
    return [
        jnp.where(chip, near[2], near[0]),
        jnp.where(chip, near[3], near[1]),
        jnp.where(chip, near[0], near[2]),
        jnp.where(chip, near[1], near[3]),
    ]


def seq_gather(values):
    far = swap(values, 2)
    return [values, swap(values, 1), far, swap(far, 1)]


def seq_reduce(parts, kind=jnp.bfloat16):
    beside = swap(parts[3].astype(kind), 1)
    across = swap((parts[2] + beside.astype(jnp.float32)).astype(kind), 2)
    close = swap(parts[1].astype(kind), 1)
    return parts[0] + close.astype(jnp.float32) + across.astype(jnp.float32)


def seq_exchange(blocks):
    return [blocks[0], swap(blocks[1], 1), swap(blocks[2], 2), swap(blocks[3], 3)]


def lines():
    count = lax.axis_size("shard")
    return [list(range(parity, count, 2)) for parity in range(2)]


def short_lines():
    return lax.axis_size("shard") // 2 <= 4


def line_gather(piece):
    return lax.all_gather(piece, "shard", axis=0, axis_index_groups=lines())


def pair_up(line, other):
    odd = (lax.axis_index("shard") & 1) == 1
    pair = jnp.stack([jnp.where(odd, other, line), jnp.where(odd, line, other)], axis=1)
    return pair.reshape((-1,) + line.shape[1:])


def shard_gather(piece):
    line = line_gather(piece)
    return pair_up(line, swap(line, 1, "shard"))


def ring_gather(piece):
    if not short_lines():
        return shard_gather(piece)
    count = lax.axis_size("shard") // 2
    at = lax.axis_index("shard") >> 1
    parity = lax.axis_index("shard") & 1
    full = jnp.zeros((count, 2) + piece.shape, piece.dtype)
    held = piece
    for step in range(count):
        other = swap(held, 1, "shard")
        spot = (at - step) % count
        full = lax.dynamic_update_slice(full, held[None, None], (spot, parity, 0, 0))
        full = lax.dynamic_update_slice(full, other[None, None], (spot, 1 - parity, 0, 0))
        if step < count - 1:
            held = ring(held)
    return full.reshape((-1,) + piece.shape)


def shard_reduce(terms):
    pair = terms.reshape((-1, 2) + terms.shape[1:])
    parity = lax.axis_index("shard") & 1
    away = lax.dynamic_index_in_dim(pair, 1 - parity, 1, keepdims=False)
    came = swap(away, 1, "shard")
    mine = lax.dynamic_index_in_dim(pair, parity, 1, keepdims=False)
    total = low(mine.astype(jnp.float32) + came.astype(jnp.float32))
    flat = total.reshape((-1,) + total.shape[2:])
    return lax.psum_scatter(
        flat, "shard", scatter_dimension=0, tiled=True, axis_index_groups=lines()
    )


def ring_reduce(terms):
    if not short_lines():
        return shard_reduce(terms)
    count = lax.axis_size("shard") // 2
    pair = terms.reshape((count, 2) + terms.shape[1:])
    at = lax.axis_index("shard") >> 1
    parity = lax.axis_index("shard") & 1

    def chunk(spot, side):
        cut = lax.dynamic_slice(pair, (spot, side, 0, 0), (1, 1) + terms.shape[1:])
        return cut[0, 0]

    total = None
    for step in range(1, count + 1):
        spot = (at - step) % count
        came = swap(chunk(spot, 1 - parity), 1, "shard")
        value = chunk(spot, parity).astype(jnp.float32) + came.astype(jnp.float32)
        if total is not None:
            value = value + ring(low(total)).astype(jnp.float32)
        total = value
    return low(total)


def shard_sum(values):
    bit = 1
    while bit < lax.axis_size("shard"):
        values = values + swap(values, bit, "shard")
        bit *= 2
    return values


def causal_scores(query_block, key_prefix, offset):
    scores = jnp.einsum(
        "qhd,khd->hqk", query_block, key_prefix, preferred_element_type=jnp.float32
    ) * HEAD ** (-0.5)
    query_pos = offset + lax.broadcasted_iota(jnp.int32, scores.shape, 1)
    key_pos = lax.broadcasted_iota(jnp.int32, scores.shape, 2)
    return jnp.where(key_pos <= query_pos, scores, MASKED)


def causal_forward(query_heads, key_heads, value_heads):
    length = query_heads.shape[0]
    block_rows = min(512, length)
    outputs = []
    log_sums = []
    for first_row in range(0, length, block_rows):
        last_row = first_row + block_rows
        scores = causal_scores(query_heads[first_row:last_row], key_heads[:last_row], first_row)
        row_peak = jnp.max(scores, axis=-1, keepdims=True)
        expd = jnp.exp(scores - row_peak)
        row_total = jnp.sum(expd, axis=-1, keepdims=True)
        probabilities = (expd / row_total).astype(jnp.bfloat16)
        outputs.append(
            jnp.einsum(
                "hqk,khd->qhd",
                probabilities,
                value_heads[:last_row],
                preferred_element_type=jnp.float32,
            )
        )
        log_sums.append(row_peak + jnp.log(row_total))
    return (jnp.concatenate(outputs, axis=0).astype(jnp.bfloat16), log_sums)


def causal_backward(query_heads, key_heads, value_heads, grad_heads, log_sums):
    length = query_heads.shape[0]
    block_rows = min(512, length)
    factor = HEAD ** (-0.5)
    query_grads = []
    key_grads = jnp.zeros(key_heads.shape, jnp.float32)
    value_grads = jnp.zeros(value_heads.shape, jnp.float32)
    for block_index, first_row in enumerate(range(0, length, block_rows)):
        last_row = first_row + block_rows
        query_block = query_heads[first_row:last_row]
        grad_block = grad_heads[first_row:last_row]
        scores = causal_scores(query_block, key_heads[:last_row], first_row)
        probabilities = jnp.exp(scores - log_sums[block_index])
        grad_probs = jnp.einsum(
            "qhd,khd->hqk", grad_block, value_heads[:last_row], preferred_element_type=jnp.float32
        )
        row_inner = jnp.sum(probabilities * grad_probs, axis=-1, keepdims=True)
        grad_scores = (probabilities * (grad_probs - row_inner)).astype(jnp.bfloat16)
        query_grads.append(
            jnp.einsum(
                "hqk,khd->qhd",
                grad_scores,
                key_heads[:last_row],
                preferred_element_type=jnp.float32,
            )
            * factor
        )
        key_grads = key_grads.at[:last_row].add(
            jnp.einsum("hqk,qhd->khd", grad_scores, query_block, preferred_element_type=jnp.float32)
            * factor
        )
        value_grads = value_grads.at[:last_row].add(
            jnp.einsum(
                "hqk,qhd->khd",
                probabilities.astype(jnp.bfloat16),
                grad_block,
                preferred_element_type=jnp.float32,
            )
        )
    return (jnp.concatenate(query_grads, axis=0), key_grads, value_grads)


def layer(
    frames,
    text_states,
    holds_clip,
    self_proj,
    self_out,
    cross_query,
    cross_keyval,
    cross_out,
    feed_in,
    feed_out,
    norm_gain,
    norm_bias,
    cotangent,
):
    seq_count = lax.axis_size("seq")
    shards = lax.axis_size("shard")
    own = lax.axis_index("seq")
    factor = HEAD ** (-0.5)
    presence = holds_clip.astype(jnp.float32)[0]
    inputs = frames[0].astype(jnp.float32)
    rows, width = inputs.shape
    group_width = width // seq_count
    head_group = group_width // HEAD
    length = rows * seq_count
    strip = self_proj.shape[0]
    units = feed_in.shape[1]
    unit_strip = units // (shards * seq_count)

    def columns(weight, parts):
        size = weight.shape[1] // (parts * seq_count)
        cuts = [
            lax.dynamic_slice_in_dim(weight, (j * seq_count + own) * size, size, 1)
            for j in range(parts)
        ]
        return low(jnp.concatenate(cuts, axis=1))

    def whole(full):
        return full.reshape(-1, full.shape[-1])

    norms = low(jnp.concatenate([norm_gain, norm_bias], axis=0))
    spread = jnp.zeros((norms.shape[0], width), norms.dtype)
    spread = lax.dynamic_update_slice_in_dim(
        spread, norms, lax.axis_index("shard") * norms.shape[1], 1
    )
    spread = shard_sum(spread).astype(jnp.float32)
    gains, shifts = spread[:3], spread[3:]
    proj_own = whole(ring_gather(columns(self_proj, 3)))
    squares = [columns(weight, 1) for weight in (self_out, cross_query, cross_out)]
    square_line = line_gather(jnp.concatenate(squares, axis=1))
    square_other = swap(square_line, 1, "shard")
    line_blocks = seq_gather(square_line)
    other_blocks = seq_gather(square_other)
    gathered = by_index(
        [whole(pair_up(line, other)) for line, other in zip(line_blocks, other_blocks)]
    )
    out_full, query_full, cross_full = (
        jnp.concatenate(
            [block[:, i * group_width : (i + 1) * group_width] for block in gathered], axis=1
        )
        for i in range(3)
    )
    keyval_own = whole(shard_gather(columns(cross_keyval, 2)))
    expand_own = whole(shard_gather(columns(feed_in, shards)))
    contract_piece = lax.dynamic_slice_in_dim(feed_out, own * unit_strip, unit_strip, 0)
    contract_own = whole(shard_gather(low(contract_piece)))

    normed_one = low(layer_norm(inputs, gains[0], shifts[0]))
    normed_one_all = jnp.concatenate(seq_gather(normed_one), axis=0)
    packed = low(product(normed_one_all, proj_own)).reshape(seq_count, rows, 3 * group_width)
    packed = jnp.concatenate(by_index([packed[b] for b in range(seq_count)]), axis=0)
    packed = packed.reshape(length, 3, head_group, HEAD)
    query_heads, key_heads, value_heads = packed[:, 0], packed[:, 1], packed[:, 2]
    heads_out, log_sums = causal_forward(query_heads, key_heads, value_heads)
    heads_out = heads_out.reshape(seq_count, rows, group_width)
    heads_out = seq_exchange(by_index([heads_out[b] for b in range(seq_count)]))
    attn_rows = jnp.concatenate(by_index(heads_out), axis=1)
    mixed_one = inputs + product(attn_rows, out_full)

    text_rows = text_states[0]
    text_all = jnp.concatenate(by_index(seq_gather(text_rows)), axis=0)
    text_count = text_all.shape[0]
    pairs = by_index(seq_gather(low(product(text_all, keyval_own))))
    text_keys = jnp.concatenate([pair[:, :group_width] for pair in pairs], axis=1)
    text_values = jnp.concatenate([pair[:, group_width:] for pair in pairs], axis=1)
    text_keys = text_keys.reshape(text_count, HEADS, HEAD)
    text_values = text_values.reshape(text_count, HEADS, HEAD)
    normed_two = low(layer_norm(mixed_one, gains[1], shifts[1]))
    cross_queries = low(product(normed_two, query_full)).reshape(rows, HEADS, HEAD)
    cross_scores = (
        jnp.einsum("qhd,khd->hqk", cross_queries, text_keys, preferred_element_type=jnp.float32)
        * factor
    )
    row_peak = jnp.max(cross_scores, axis=-1, keepdims=True)
    expd = jnp.exp(cross_scores - row_peak)
    cross_probs = expd / jnp.sum(expd, axis=-1, keepdims=True)
    cross_rounded = low(cross_probs)
    cross_heads = low(
        jnp.einsum("hqk,khd->qhd", cross_rounded, text_values, preferred_element_type=jnp.float32)
    ).reshape(rows, width)
    mixed_two = mixed_one + product(cross_heads, cross_full)

    normed_three = low(layer_norm(mixed_two, gains[2], shifts[2]))
    blocks = seq_gather(normed_three)
    normed_three_all = [
        jnp.concatenate(blocks[:2], axis=0),
        jnp.concatenate(blocks[2:], axis=0),
    ]
    hidden_pre = [product(half, expand_own) for half in normed_three_all]
    hidden = [low(gelu_exact(half)) for half in hidden_pre]
    results = [product(half, contract_own) for half in hidden]
    parts = [results[0][:rows], results[0][rows:], results[1][:rows], results[1][rows:]]
    result = mixed_two + seq_reduce(parts)
    block_out = low(presence * result)[None]

    grad_block = low(presence * cotangent[0].astype(jnp.float32))
    grad_result = grad_block.astype(jnp.float32)
    blocks = seq_gather(grad_block)
    grad_block_all = [
        jnp.concatenate(blocks[:2], axis=0),
        jnp.concatenate(blocks[2:], axis=0),
    ]
    grad_pre = []
    for index in (0, 1):
        grad_hidden = transposed_right(grad_block_all[index], contract_own)
        gelu_pull = jax.vjp(gelu_exact, hidden_pre[index])[1]
        grad_pre.append(low(gelu_pull(grad_hidden)[0]))
    results = [transposed_right(half, expand_own) for half in grad_pre]
    parts = [results[0][:rows], results[0][rows:], results[1][:rows], results[1][rows:]]
    grad_normed = seq_reduce(parts)
    contract_term = low(
        transposed_left(jnp.concatenate(hidden, axis=0), jnp.concatenate(grad_block_all, axis=0))
    )
    expand_term = low(
        transposed_left(
            jnp.concatenate(normed_three_all, axis=0), jnp.concatenate(grad_pre, axis=0)
        )
    )
    contract_share = shard_reduce(contract_term.reshape(shards, unit_strip, width))
    expand_share = shard_reduce(expand_term.reshape(shards, strip, -1))
    norm_pull = jax.vjp(layer_norm, mixed_two, gains[2], shifts[2])[1]
    grad_mixed, gain_three, shift_three = norm_pull(grad_normed)
    grad_two = grad_result + grad_mixed

    def square_share(left, right):
        cut = [right[:, j * group_width : (j + 1) * group_width] for j in range(seq_count)]
        cut = by_index(cut)
        quarter = seq_reduce([transposed_left(left, block) for block in cut])
        return shard_reduce(low(quarter).reshape(shards, strip, group_width))

    grad_cross = low(grad_two)
    cross_share = square_share(cross_heads, grad_cross)
    grad_heads_two = low(transposed_right(grad_cross, cross_full)).reshape(rows, HEADS, HEAD)
    grad_probs = jnp.einsum(
        "qhd,khd->hqk", grad_heads_two, text_values, preferred_element_type=jnp.float32
    )
    row_inner = jnp.sum(cross_probs * grad_probs, axis=-1, keepdims=True)
    grad_scores = low(cross_probs * (grad_probs - row_inner))
    grad_queries = low(
        jnp.einsum("hqk,khd->qhd", grad_scores, text_keys, preferred_element_type=jnp.float32)
        * factor
    ).reshape(rows, width)
    grad_text_keys = (
        jnp.einsum("hqk,qhd->khd", grad_scores, cross_queries, preferred_element_type=jnp.float32)
        * factor
    ).reshape(text_count, width)
    grad_text_values = jnp.einsum(
        "hqk,qhd->khd", cross_rounded, grad_heads_two, preferred_element_type=jnp.float32
    ).reshape(text_count, width)
    cut = [
        jnp.concatenate(
            [
                grad_text_keys[:, j * group_width : (j + 1) * group_width],
                grad_text_values[:, j * group_width : (j + 1) * group_width],
            ],
            axis=1,
        )
        for j in range(seq_count)
    ]
    own_pairs = low(seq_reduce(by_index(cut), jnp.float32))
    text_term = transposed_right(own_pairs, keyval_own).reshape(seq_count, -1, width)
    text_grad = seq_reduce(by_index([text_term[b] for b in range(seq_count)]), jnp.float32)
    keyval_term = transposed_left(text_all, own_pairs)
    keyval_share = shard_reduce(low(keyval_term).reshape(shards, strip, -1))
    query_share = square_share(normed_two, grad_queries)
    norm_pull = jax.vjp(layer_norm, mixed_one, gains[1], shifts[1])[1]
    grad_normed = transposed_right(grad_queries, query_full)
    grad_mixed, gain_two, shift_two = norm_pull(grad_normed)
    grad_one = grad_two + grad_mixed

    grad_attn = low(grad_one)
    out_share = square_share(attn_rows, grad_attn)
    grad_rows = low(transposed_right(grad_attn, out_full))
    cut = [grad_rows[:, j * group_width : (j + 1) * group_width] for j in range(seq_count)]
    grad_heads = jnp.concatenate(by_index(seq_exchange(by_index(cut))), axis=0)
    grad_heads = grad_heads.reshape(length, head_group, HEAD)
    query_grad, key_grad, value_grad = causal_backward(
        query_heads, key_heads, value_heads, grad_heads, log_sums
    )
    grad_packed = low(jnp.stack([query_grad, key_grad, value_grad], axis=1))
    grad_packed = grad_packed.reshape(seq_count, rows, 3 * group_width)
    grad_packed = jnp.concatenate(by_index([grad_packed[b] for b in range(seq_count)]), axis=0)
    proj_term = low(transposed_left(normed_one_all, grad_packed))
    proj_share = ring_reduce(proj_term.reshape(shards, strip, -1))
    parts = transposed_right(grad_packed, proj_own).reshape(seq_count, rows, width)
    grad_normed = seq_reduce([parts[b] for b in range(seq_count)])
    norm_pull = jax.vjp(layer_norm, inputs, gains[0], shifts[0])[1]
    grad_mixed, gain_one, shift_one = norm_pull(grad_normed)
    frames_grad = (grad_one + grad_mixed)[None]

    norm_terms = jnp.stack([gain_one, gain_two, gain_three, shift_one, shift_two, shift_three])
    norm_terms = norm_terms + swap(norm_terms, 1)
    norm_terms = norm_terms + swap(norm_terms, 2)
    norm_terms = shard_sum(norm_terms)
    norm_terms = lax.dynamic_slice_in_dim(
        norm_terms, lax.axis_index("shard") * strip, strip, 1
    )

    def filled(share, parts):
        blocks = by_index(seq_gather(share))
        size = share.shape[1] // parts
        cuts = [
            block[:, j * size : (j + 1) * size] for j in range(parts) for block in blocks
        ]
        return jnp.concatenate(cuts, axis=1).astype(jnp.float32)

    feed_out_grad = jnp.concatenate(
        by_index(seq_gather(contract_share)), axis=0
    ).astype(jnp.float32)
    return (
        block_out,
        frames_grad,
        text_grad[None],
        filled(proj_share, 3),
        filled(out_share, 1),
        filled(query_share, 1),
        filled(keyval_share, 2),
        filled(cross_share, 1),
        filled(expand_share, shards),
        feed_out_grad,
        norm_terms[:3],
        norm_terms[3:],
    )


def solution(mesh):
    in_specs = (
        P("shard", "seq", None),
        P("shard", "seq", None),
        P("shard"),
        P("shard", None),
        P("shard", None),
        P("shard", None),
        P("shard", None),
        P("shard", None),
        P("shard", None),
        P("shard", None),
        P(None, "shard"),
        P(None, "shard"),
        P("shard", "seq", None),
    )
    out_specs = (
        P("shard", "seq", None),
        P("shard", "seq", None),
        P("shard", "seq", None),
        P("shard", None),
        P("shard", None),
        P("shard", None),
        P("shard", None),
        P("shard", None),
        P("shard", None),
        P("shard", None),
        P(None, "shard"),
        P(None, "shard"),
    )

    return jax.shard_map(layer, mesh=mesh, in_specs=in_specs, out_specs=out_specs, check_vma=False)
```

```python
import jax
import jax.numpy as jnp
from jax import lax
from jax.sharding import PartitionSpec as P


SEQ = "seq"
SHARD = "shard"
SCORES = "qhd,khd->hqk"
MIX = "hqk,khd->qhd"
BACK = "hqk,qhd->khd"
HEADS = 24
HEAD = 64


EPSILON = 1e-05
MASKED = -1e30


def layer_norm(values, gain_row, shift_row):
    centre = values - jnp.mean(values, axis=-1, keepdims=True)
    spread = jnp.mean(centre * centre, axis=-1, keepdims=True)
    return centre * lax.rsqrt(spread + EPSILON) * gain_row + shift_row


def gelu_exact(values):
    return jax.nn.gelu(values, approximate=False)


def product(left, right):
    return jnp.dot(left, right, preferred_element_type=jnp.float32)


def transposed_left(left, right):
    return lax.dot_general(
        left, right, (((0,), (0,)), ((), ())), preferred_element_type=jnp.float32
    )


def transposed_right(left, right):
    return lax.dot_general(
        left, right, (((1,), (1,)), ((), ())), preferred_element_type=jnp.float32
    )


def low(values):
    return values.astype(jnp.bfloat16)


def swap(values, bit, axis=SEQ):
    count = lax.axis_size(axis)
    return lax.ppermute(values, axis, [(i, i ^ bit) for i in range(count)])


def ring(values):
    count = lax.axis_size(SHARD)
    return lax.ppermute(values, SHARD, [(i, (i + 2) % count) for i in range(count)])


def by_index(blocks):
    own = lax.axis_index(SEQ)
    core = (own & 1) == 1
    chip = (own & 2) == 2
    near = [
        jnp.where(core, blocks[1], blocks[0]),
        jnp.where(core, blocks[0], blocks[1]),
        jnp.where(core, blocks[3], blocks[2]),
        jnp.where(core, blocks[2], blocks[3]),
    ]
    return [
        jnp.where(chip, near[2], near[0]),
        jnp.where(chip, near[3], near[1]),
        jnp.where(chip, near[0], near[2]),
        jnp.where(chip, near[1], near[3]),
    ]


def seq_gather(values):
    far = swap(values, 2)
    return [values, swap(values, 1), far, swap(far, 1)]


def seq_reduce(parts, kind=jnp.bfloat16):
    beside = swap(parts[3].astype(kind), 1)
    across = swap((parts[2] + beside.astype(jnp.float32)).astype(kind), 2)
    close = swap(parts[1].astype(kind), 1)
    return parts[0] + close.astype(jnp.float32) + across.astype(jnp.float32)


def seq_exchange(blocks):
    return [blocks[0], swap(blocks[1], 1), swap(blocks[2], 2), swap(blocks[3], 3)]


def lines():
    count = lax.axis_size(SHARD)
    return [list(range(parity, count, 2)) for parity in range(2)]


def short_lines():
    return lax.axis_size(SHARD) // 2 <= 4


def line_gather(piece):
    return lax.all_gather(piece, SHARD, axis=0, axis_index_groups=lines())


def pair_up(line, other):
    odd = (lax.axis_index(SHARD) & 1) == 1
    pair = jnp.stack([jnp.where(odd, other, line), jnp.where(odd, line, other)], axis=1)
    return pair.reshape((-1,) + line.shape[1:])


def pair_across(line):
    return pair_up(line, swap(line, 1, SHARD))


def shard_gather(piece):
    return pair_across(line_gather(piece))


def shard_gather_across(piece):
    full = line_gather(pair_across(piece[None]))
    return full.reshape((-1,) + piece.shape)


def ring_gather(piece, split):
    if not short_lines():
        full = shard_gather(piece)
        return full[:, :split], full[:, split:]
    count = lax.axis_size(SHARD) // 2
    at = lax.axis_index(SHARD) >> 1
    parity = lax.axis_index(SHARD) & 1
    top = jnp.zeros((count, 2, split, piece.shape[1]), piece.dtype)
    rest = jnp.zeros((count, 2, piece.shape[0] - split, piece.shape[1]), piece.dtype)
    held = piece
    for step in range(count):
        other = swap(held, 1, SHARD)
        spot = (at - step) % count
        for block, side in ((held, parity), (other, 1 - parity)):
            top = lax.dynamic_update_slice(top, block[None, None, :split], (spot, side, 0, 0))
            rest = lax.dynamic_update_slice(rest, block[None, None, split:], (spot, side, 0, 0))
        if step < count - 1:
            held = ring(held)
    return top.reshape((-1,) + top.shape[2:]), rest.reshape((-1,) + rest.shape[2:])


def shard_reduce(terms):
    pair = terms.reshape((-1, 2) + terms.shape[1:])
    parity = lax.axis_index(SHARD) & 1
    away = lax.dynamic_index_in_dim(pair, 1 - parity, 1, keepdims=False)
    came = swap(away, 1, SHARD)
    mine = lax.dynamic_index_in_dim(pair, parity, 1, keepdims=False)
    total = low(mine.astype(jnp.float32) + came.astype(jnp.float32))
    flat = total.reshape((-1,) + total.shape[2:])
    return line_reduce(flat)


def line_reduce(flat):
    return lax.psum_scatter(flat, SHARD, scatter_dimension=0, tiled=True, axis_index_groups=lines())


def shard_reduce_along(terms):
    pair = line_reduce(terms.reshape((-1,) + terms.shape[2:]))
    pair = pair.reshape((2,) + terms.shape[1:])
    parity = lax.axis_index(SHARD) & 1
    away = lax.dynamic_index_in_dim(pair, 1 - parity, 0, keepdims=False)
    came = swap(away, 1, SHARD)
    mine = lax.dynamic_index_in_dim(pair, parity, 0, keepdims=False)
    return low(mine.astype(jnp.float32) + came.astype(jnp.float32))


def ring_reduce(terms):
    if not short_lines():
        return shard_reduce(terms)
    count = lax.axis_size(SHARD) // 2
    pair = terms.reshape((count, 2) + terms.shape[1:])
    at = lax.axis_index(SHARD) >> 1
    parity = lax.axis_index(SHARD) & 1

    def chunk(spot, side):
        cut = lax.dynamic_slice(pair, (spot, side, 0, 0), (1, 1) + terms.shape[1:])
        return cut[0, 0]

    total = None
    for step in range(1, count + 1):
        spot = (at - step) % count
        came = swap(chunk(spot, 1 - parity), 1, SHARD)
        value = chunk(spot, parity).astype(jnp.float32) + came.astype(jnp.float32)
        if total is not None:
            value = value + ring(low(total)).astype(jnp.float32)
        total = value
    return low(total)


def shard_sum(values):
    bit = 1
    while bit < lax.axis_size(SHARD):
        values = values + swap(values, bit, SHARD)
        bit *= 2
    return values


def causal_scores(query_block, key_prefix, offset):
    scores = jnp.einsum(
        SCORES, query_block, key_prefix, preferred_element_type=jnp.float32
    ) * HEAD ** (-0.5)
    query_pos = offset + lax.broadcasted_iota(jnp.int32, scores.shape, 1)
    key_pos = lax.broadcasted_iota(jnp.int32, scores.shape, 2)
    return jnp.where(key_pos <= query_pos, scores, MASKED)


def causal_forward(query_heads, key_heads, value_heads):
    length = query_heads.shape[0]
    block_rows = min(512, length)
    outputs = []
    log_sums = []
    for first_row in range(0, length, block_rows):
        last_row = first_row + block_rows
        scores = causal_scores(query_heads[first_row:last_row], key_heads[:last_row], first_row)
        row_peak = jnp.max(scores, axis=-1, keepdims=True)
        expd = jnp.exp(scores - row_peak)
        row_total = jnp.sum(expd, axis=-1, keepdims=True)
        probabilities = (expd / row_total).astype(jnp.bfloat16)
        outputs.append(
            jnp.einsum(
                MIX,
                probabilities,
                value_heads[:last_row],
                preferred_element_type=jnp.float32,
            )
        )
        log_sums.append(row_peak + jnp.log(row_total))
    return (jnp.concatenate(outputs, axis=0).astype(jnp.bfloat16), log_sums)


def causal_backward(query_heads, key_heads, value_heads, grad_heads, log_sums):
    length = query_heads.shape[0]
    block_rows = min(512, length)
    factor = HEAD ** (-0.5)
    query_grads = []
    key_grads = jnp.zeros(key_heads.shape, jnp.float32)
    value_grads = jnp.zeros(value_heads.shape, jnp.float32)
    for block_index, first_row in enumerate(range(0, length, block_rows)):
        last_row = first_row + block_rows
        query_block = query_heads[first_row:last_row]
        grad_block = grad_heads[first_row:last_row]
        scores = causal_scores(query_block, key_heads[:last_row], first_row)
        probabilities = jnp.exp(scores - log_sums[block_index])
        grad_probs = jnp.einsum(
            SCORES, grad_block, value_heads[:last_row], preferred_element_type=jnp.float32
        )
        row_inner = jnp.sum(probabilities * grad_probs, axis=-1, keepdims=True)
        grad_scores = (probabilities * (grad_probs - row_inner)).astype(jnp.bfloat16)
        query_grads.append(
            jnp.einsum(MIX, grad_scores, key_heads[:last_row], preferred_element_type=jnp.float32)
            * factor
        )
        key_grads = key_grads.at[:last_row].add(
            jnp.einsum(BACK, grad_scores, query_block, preferred_element_type=jnp.float32)
            * factor
        )
        value_grads = value_grads.at[:last_row].add(
            jnp.einsum(
                BACK,
                probabilities.astype(jnp.bfloat16),
                grad_block,
                preferred_element_type=jnp.float32,
            )
        )
    return (jnp.concatenate(query_grads, axis=0), key_grads, value_grads)


def layer(
    frames,
    text_states,
    holds_clip,
    self_proj,
    self_out,
    cross_query,
    cross_keyval,
    cross_out,
    feed_in,
    feed_out,
    norm_gain,
    norm_bias,
    cotangent,
):
    seq_count = lax.axis_size(SEQ)
    shards = lax.axis_size(SHARD)
    own = lax.axis_index(SEQ)
    factor = HEAD ** (-0.5)
    presence = holds_clip.astype(jnp.float32)[0]
    inputs = frames[0].astype(jnp.float32)
    rows, width = inputs.shape
    group_width = width // seq_count
    head_group = group_width // HEAD
    length = rows * seq_count
    strip = self_proj.shape[0]
    units = feed_in.shape[1]
    unit_strip = units // (shards * seq_count)

    def columns(weight, parts):
        size = weight.shape[1] // (parts * seq_count)
        cuts = [
            lax.dynamic_slice_in_dim(weight, (j * seq_count + own) * size, size, 1)
            for j in range(parts)
        ]
        return low(jnp.concatenate(cuts, axis=1))

    def whole(full):
        return full.reshape(-1, full.shape[-1])

    norms = low(jnp.concatenate([norm_gain, norm_bias], axis=0)).reshape(-1)
    piece = columns(self_proj, 3)
    extra = -(-norms.shape[0] // piece.shape[1])
    norms = jnp.pad(norms, (0, extra * piece.shape[1] - norms.shape[0]))
    piece = jnp.concatenate([piece, norms.reshape(extra, -1)], axis=0)
    proj_own, spread = ring_gather(piece, strip)
    proj_own = whole(proj_own)
    spread = spread.reshape(shards, -1)[:, : 6 * norm_gain.shape[1]]
    spread = jnp.swapaxes(spread.reshape(shards, 6, -1), 0, 1).reshape(6, width)
    spread = spread.astype(jnp.float32)
    gains, shifts = spread[:3], spread[3:]
    squares = jnp.stack([columns(weight, 1) for weight in (self_out, cross_query, cross_out)])
    squares = line_gather(squares)
    out_blocks, query_blocks, cross_blocks = (
        seq_gather(whole(pair_across(squares[:, i])))
        for i in range(3)
    )
    keyval_own = whole(shard_gather(columns(cross_keyval, 2)))
    expand_own = whole(shard_gather(columns(feed_in, shards)))
    contract_piece = lax.dynamic_slice_in_dim(feed_out, own * unit_strip, unit_strip, 0)
    contract_own = whole(shard_gather_across(low(contract_piece)))

    def groups(values):
        return by_index(
            [values[:, j * group_width : (j + 1) * group_width] for j in range(seq_count)]
        )

    def spread_product(values, blocks):
        return jnp.concatenate(by_index([product(values, block) for block in blocks]), axis=1)

    def pull_product(cuts, blocks):
        return sum(transposed_right(cut, block) for cut, block in zip(cuts, blocks))

    frames_all = jnp.concatenate(seq_gather(frames[0]), axis=0).astype(jnp.float32)
    normed_one_all = low(layer_norm(frames_all, gains[0], shifts[0]))
    packed = low(product(normed_one_all, proj_own)).reshape(seq_count, rows, 3 * group_width)
    packed = jnp.concatenate(by_index([packed[b] for b in range(seq_count)]), axis=0)
    packed = packed.reshape(length, 3, head_group, HEAD)
    query_heads, key_heads, value_heads = packed[:, 0], packed[:, 1], packed[:, 2]
    heads_out, log_sums = causal_forward(query_heads, key_heads, value_heads)
    heads_out = heads_out.reshape(seq_count, rows, group_width)
    heads_out = seq_exchange(by_index([heads_out[b] for b in range(seq_count)]))
    attn_rows = jnp.concatenate(by_index(heads_out), axis=1)
    mixed_one = inputs + spread_product(attn_rows, out_blocks)

    text_rows = text_states[0]
    text_all = jnp.concatenate(by_index(seq_gather(text_rows)), axis=0)
    text_count = text_all.shape[0]
    pairs = seq_gather(low(product(text_all, keyval_own)))
    text_keys = jnp.concatenate([pair[:, :group_width] for pair in pairs], axis=1)
    text_values = jnp.concatenate([pair[:, group_width:] for pair in pairs], axis=1)
    text_keys = text_keys.reshape(text_count, HEADS, HEAD)
    text_values = text_values.reshape(text_count, HEADS, HEAD)
    normed_two = low(layer_norm(mixed_one, gains[1], shifts[1]))
    cross_queries = low(
        jnp.concatenate([product(normed_two, block) for block in query_blocks], axis=1)
    ).reshape(rows, HEADS, HEAD)
    cross_scores = (
        jnp.einsum(SCORES, cross_queries, text_keys, preferred_element_type=jnp.float32)
        * factor
    )
    row_peak = jnp.max(cross_scores, axis=-1, keepdims=True)
    expd = jnp.exp(cross_scores - row_peak)
    cross_probs = expd / jnp.sum(expd, axis=-1, keepdims=True)
    cross_rounded = low(cross_probs)
    cross_heads = low(
        jnp.einsum(MIX, cross_rounded, text_values, preferred_element_type=jnp.float32)
    ).reshape(rows, width)
    cross_heads = jnp.concatenate(groups(cross_heads), axis=1)
    mixed_two = mixed_one + spread_product(cross_heads, cross_blocks)

    normed_three = low(layer_norm(mixed_two, gains[2], shifts[2]))
    blocks = seq_gather(normed_three)
    normed_three_all = [
        jnp.concatenate(blocks[:2], axis=0),
        jnp.concatenate(blocks[2:], axis=0),
    ]
    hidden_pre, hidden, results = [], [], []
    for index, half in enumerate(normed_three_all):
        hidden_pre.append(product(half, expand_own))
        hidden.append(low(gelu_exact(hidden_pre[index])))
        results.append(product(hidden[index], contract_own))
    parts = [results[0][:rows], results[0][rows:], results[1][:rows], results[1][rows:]]
    result = seq_reduce(parts)

    live = low(presence)
    grad_result = presence * cotangent[0].astype(jnp.float32)
    blocks = [live * block for block in seq_gather(cotangent[0])]
    grad_block_all = [
        jnp.concatenate(blocks[:2], axis=0),
        jnp.concatenate(blocks[2:], axis=0),
    ]
    grad_pre = []
    for index in (0, 1):
        grad_hidden = transposed_right(grad_block_all[index], contract_own)
        gelu_pull = jax.vjp(gelu_exact, hidden_pre[index])[1]
        grad_pre.append(low(gelu_pull(grad_hidden)[0]))
    results = []
    for half in grad_pre:
        results.append(transposed_right(half, expand_own))
    parts = [results[0][:rows], results[0][rows:], results[1][:rows], results[1][rows:]]
    grad_normed = seq_reduce(parts)
    contract_term = low(
        transposed_left(jnp.concatenate(hidden, axis=0), jnp.concatenate(grad_block_all, axis=0))
    )
    expand_term = low(
        transposed_left(
            jnp.concatenate(normed_three_all, axis=0), jnp.concatenate(grad_pre, axis=0)
        )
    )
    contract_share = shard_reduce_along(contract_term.reshape(shards, unit_strip, width))
    expand_share = shard_reduce(expand_term.reshape(shards, strip, -1))
    norm_pull = jax.vjp(layer_norm, mixed_two, gains[2], shifts[2])[1]
    grad_mixed, gain_three, shift_three = norm_pull(grad_normed)
    grad_two = grad_result + grad_mixed

    def square_quarter(left, cut):
        return low(seq_reduce([transposed_left(left, block) for block in cut]))

    grad_cross = groups(low(grad_two))
    cross_quarter = square_quarter(cross_heads, grad_cross)
    grad_heads_two = low(pull_product(grad_cross, cross_blocks))
    grad_heads_two = jnp.concatenate(groups(grad_heads_two), axis=1).reshape(rows, HEADS, HEAD)
    grad_probs = jnp.einsum(
        SCORES, grad_heads_two, text_values, preferred_element_type=jnp.float32
    )
    row_inner = jnp.sum(cross_probs * grad_probs, axis=-1, keepdims=True)
    grad_scores = low(cross_probs * (grad_probs - row_inner))
    grad_queries = low(
        jnp.einsum(MIX, grad_scores, text_keys, preferred_element_type=jnp.float32)
        * factor
    ).reshape(rows, width)
    grad_text_keys = (
        jnp.einsum(BACK, grad_scores, cross_queries, preferred_element_type=jnp.float32)
        * factor
    ).reshape(text_count, width)
    grad_text_values = jnp.einsum(
        BACK, cross_rounded, grad_heads_two, preferred_element_type=jnp.float32
    ).reshape(text_count, width)
    cut = [
        jnp.concatenate(
            [
                grad_text_keys[:, j * group_width : (j + 1) * group_width],
                grad_text_values[:, j * group_width : (j + 1) * group_width],
            ],
            axis=1,
        )
        for j in range(seq_count)
    ]
    own_pairs = low(seq_reduce(cut, jnp.float32))
    text_term = transposed_right(own_pairs, keyval_own).reshape(seq_count, -1, width)
    text_grad = seq_reduce(by_index([text_term[b] for b in range(seq_count)]), jnp.float32)
    keyval_term = low(transposed_left(text_all, own_pairs))
    grad_queries = [
        grad_queries[:, j * group_width : (j + 1) * group_width] for j in range(seq_count)
    ]
    query_quarter = square_quarter(normed_two, grad_queries)
    cross_pair = jnp.concatenate([keyval_term, cross_quarter], axis=1)
    cross_share = shard_reduce(cross_pair.reshape(shards, strip, -1))
    norm_pull = jax.vjp(layer_norm, mixed_one, gains[1], shifts[1])[1]
    grad_normed = pull_product(grad_queries, query_blocks)
    grad_mixed, gain_two, shift_two = norm_pull(grad_normed)
    grad_one = grad_two + grad_mixed

    grad_one, mixed_late = lax.optimization_barrier((grad_one, mixed_two))
    block_out = low(presence * (mixed_late + result))[None]
    grad_attn = groups(low(grad_one))
    out_quarter = square_quarter(attn_rows, grad_attn)
    out_pair = jnp.concatenate([query_quarter, out_quarter], axis=1)
    out_share = shard_reduce(out_pair.reshape(shards, strip, -1))
    grad_rows = low(pull_product(grad_attn, out_blocks))
    grad_heads = jnp.concatenate(by_index(seq_exchange(groups(grad_rows))), axis=0)
    grad_heads = grad_heads.reshape(length, head_group, HEAD)
    query_grad, key_grad, value_grad = causal_backward(
        query_heads, key_heads, value_heads, grad_heads, log_sums
    )
    grad_packed = low(jnp.stack([query_grad, key_grad, value_grad], axis=1))
    grad_packed = grad_packed.reshape(seq_count, rows, 3 * group_width)
    grad_packed = jnp.concatenate(by_index([grad_packed[b] for b in range(seq_count)]), axis=0)
    proj_term = low(transposed_left(normed_one_all, grad_packed))
    proj_share = ring_reduce(proj_term.reshape(shards, strip, -1))
    parts = transposed_right(grad_packed, proj_own).reshape(seq_count, rows, width)
    grad_normed = seq_reduce([parts[b] for b in range(seq_count)])
    norm_pull = jax.vjp(layer_norm, inputs, gains[0], shifts[0])[1]
    grad_mixed, gain_one, shift_one = norm_pull(grad_normed)
    frames_grad = (grad_one + grad_mixed)[None]

    norm_terms = jnp.stack([gain_one, gain_two, gain_three, shift_one, shift_two, shift_three])
    norm_terms = norm_terms + swap(norm_terms, 1)
    norm_terms = norm_terms + swap(norm_terms, 2)
    norm_terms = shard_sum(norm_terms)
    norm_terms = lax.dynamic_slice_in_dim(
        norm_terms, lax.axis_index(SHARD) * strip, strip, 1
    )

    def filled(blocks, parts):
        size = blocks[0].shape[1] // parts
        cuts = [
            block[:, j * size : (j + 1) * size] for j in range(parts) for block in blocks
        ]
        return jnp.concatenate(cuts, axis=1).astype(jnp.float32)

    feed_out_grad = jnp.concatenate(
        by_index(seq_gather(contract_share)), axis=0
    ).astype(jnp.float32)
    expand_blocks = by_index(seq_gather(expand_share))
    cross_filled = by_index(seq_gather(cross_share))
    out_filled = by_index(seq_gather(out_share))
    keyval_grad = filled([block[:, : 2 * group_width] for block in cross_filled], 2)
    cross_grad = filled([block[:, 2 * group_width :] for block in cross_filled], 1)
    query_grad = filled([block[:, :group_width] for block in out_filled], 1)
    out_grad = filled([block[:, group_width:] for block in out_filled], 1)
    return (
        block_out,
        frames_grad,
        text_grad[None],
        filled(by_index(seq_gather(proj_share)), 3),
        out_grad,
        query_grad,
        keyval_grad,
        cross_grad,
        filled(expand_blocks, shards),
        feed_out_grad,
        norm_terms[:3],
        norm_terms[3:],
    )


def solution(mesh):
    rows = P(SHARD, SEQ, None)
    weight = P(SHARD, None)
    norm = P(None, SHARD)
    in_specs = (rows, rows, P(SHARD)) + (weight,) * 7 + (norm, norm, rows)
    out_specs = (rows,) * 3 + (weight,) * 7 + (norm, norm)

    return jax.shard_map(layer, mesh=mesh, in_specs=in_specs, out_specs=out_specs, check_vma=False)
```
